512 devices in a mesh: ctx: 64 (over z, y), mod: 8 (over x, core).
Axes of the slice: x: 4, y: 8, z: 8, core: 2. Of those that a mesh axis runs over, the one named last changes fastest.
Arguments:
- seq_input: float32 [8192, 4096], P('ctx', 'mod'), may hold values from -6 to 6
- log_decay: float32 [64, 8192], P('mod', 'ctx'), may hold values from -0.7 to 0
- b_proj: float32 [8192, 128], P('ctx'), may hold values from -0.2 to 0.2
- c_proj: float32 [8192, 128], P('ctx'), may hold values from -0.2 to 0.2
- skip_gain: float32 [64], P('mod'), may hold values from 0.1 to 1.9
- down_weight: float32 [2, 4096, 256], P(None, 'mod'), may hold values from -0.09375 to 0.09375
- up_weight: float32 [2, 256, 4096], P(None, None, 'mod'), may hold values from -0.375 to 0.375
- block_lang: int32 [64], P('ctx'), may hold values from 0 to 1
- cotangent: float32 [8192, 4096], P('ctx', 'mod'), may hold values from -6 to 6
Outputs:
- layer_out: float32 [8192, 4096], P('ctx', 'mod')
- input_grad: float32 [8192, 4096], P('ctx', 'mod')
- b_grad: float32 [8192, 128], P('ctx')
- c_grad: float32 [8192, 128], P('ctx')
- down_grad: float32 [2, 4096, 256], P(None, 'mod', 'ctx')
- up_grad: float32 [2, 256, 4096], P(None, 'ctx', 'mod')
The draws below stay inside these ranges and needn't reach their ends.
All inputs are finite; a program needn't handle non-finite values.
Results may differ from the reference program's by a relative error of at most 0.0003.
Values sent between devices are 32-bit elements; how exact they have to be, the bound alone decides.
A program may use at most 128 MiB of HBM per device.

```python
import jax
import jax.numpy as jnp
from jax import lax

HEAD_GROUP = 64
P_SIZE = 64
N = 128
R = 256
LANG = 2
BLK = 128
TOK_DEV = 128
TOKEN_WINDOW = 8192
FEAT = 4096


def draw_log_decay(key, part):
    quick_key, rate_key, gradual_key, noise_key, spike_key, depth_key = jax.random.split(key, 6)
    fast_share = 0.5
    fast_heads = jax.random.bernoulli(quick_key, fast_share, (HEAD_GROUP, 1))
    fast_rate = -1.0 / jax.random.uniform(rate_key, (HEAD_GROUP, 1), jnp.float32, 30.0, 50.0)
    slow_rate = -jnp.exp(jax.random.uniform(gradual_key, (HEAD_GROUP, 1), jnp.float32, -2.3, 0.0)) / TOKEN_WINDOW
    baseline_rate = jnp.where(fast_heads, fast_rate, slow_rate)
    jitter_noise = jnp.exp(jax.random.uniform(noise_key, (HEAD_GROUP, TOKEN_WINDOW), jnp.float32, -0.69, 0.69))
    spike_events = jax.random.bernoulli(spike_key, 3.0 / TOKEN_WINDOW, (HEAD_GROUP, TOKEN_WINDOW))
    spike_value = jnp.log(jax.random.uniform(depth_key, (HEAD_GROUP, TOKEN_WINDOW), jnp.float32, 0.5, 0.8))
    return jnp.where(spike_events, spike_value, baseline_rate * jitter_noise).astype(jnp.float32)


def set_ends(result, stream_key, least, top_value):
    dims = result.shape
    spot = [jax.random.randint(jax.random.fold_in(stream_key, axis), (), 0, dims[axis]) for axis in range(len(dims))]
    result = result.at[tuple(spot)].set(least)
    longest = dims.index(max(dims))
    spot[longest] = (spot[longest] + 1) % dims[longest]
    return result.at[tuple(spot)].set(top_value)


def block_levels(stream_key, shape, cuts, least, top_value):
    level = 1.0
    for dim, parts in cuts:
        heights = jax.random.uniform(jax.random.fold_in(jax.random.fold_in(stream_key, 6), dim), (parts,), jnp.float32, least / len(cuts), top_value / len(cuts))
        level = level * jnp.repeat(jnp.exp(heights), shape[dim] // parts).reshape((-1,) + (1,) * (len(shape) - 1 - dim))
    return level


def normal_values(key, shape, scale, most, cuts=(), kind=jnp.bfloat16):
    loudness = block_levels(key, shape, cuts, -0.22, 0.18) if cuts else 1.0
    entries = jax.random.normal(key, shape, jnp.float32) * scale * loudness
    return jnp.minimum(jnp.maximum(entries, -most), most).astype(kind)


def setup_inputs(seed: int = 0) -> dict:
    key_list = jax.random.split(jax.random.key(seed), 10)
    return {
        "seq_input": normal_values(key_list[0], (TOKEN_WINDOW, FEAT), 1.0, 6.0, ((0, 64), (1, 8)), jnp.float32),
        "log_decay": draw_log_decay(jax.random.fold_in(key_list[9], 71), 0),
        "b_proj": normal_values(key_list[2], (TOKEN_WINDOW, N), 0.03, 0.2, ((0, 64),), jnp.float32),
        "c_proj": normal_values(key_list[3], (TOKEN_WINDOW, N), 0.03, 0.2, ((0, 64),), jnp.float32),
        "skip_gain": jnp.clip(1.0 + 0.18 * jax.random.normal(key_list[4], (HEAD_GROUP,), jnp.float32), 0.1, 1.9),
        "down_weight": normal_values(key_list[5], (LANG, FEAT, R), FEAT ** -0.5, 0.09375, ((1, 8),), jnp.float32),
        "up_weight": normal_values(key_list[6], (LANG, R, FEAT), R ** -0.5, 0.375, ((2, 8),), jnp.float32),
        "block_lang": set_ends(jax.random.randint(key_list[7], (TOKEN_WINDOW // BLK,), 0, LANG), jax.random.fold_in(key_list[7], 1), 0, LANG - 1).astype(jnp.int32),
        "cotangent": normal_values(key_list[8], (TOKEN_WINDOW, FEAT), 1.0, 6.0, ((0, 64), (1, 8)), jnp.float32),
    }


highest = lax.Precision.HIGHEST

def group_free_scan(seq_in, log_decay, b_in, c_in, skip_gain):
    block_len = TOK_DEV
    block_count = TOKEN_WINDOW // block_len
    x_blocks = seq_in.reshape(block_count, block_len, HEAD_GROUP, P_SIZE)
    d_blocks = log_decay.reshape(HEAD_GROUP, block_count, block_len).transpose(1, 0, 2)
    b_blocks = b_in.reshape(block_count, block_len, N)
    c_blocks = c_in.reshape(block_count, block_len, N)
    lower_mask = jnp.tril(jnp.ones((block_len, block_len), bool))

    def advance(state, pieces):
        x_blk, ld_blk, b_blk, c_blk = pieces
        cumulative = jnp.cumsum(ld_blk, axis=1)
        gaps = cumulative[:, :, None] - cumulative[:, None, :]
        decay_mask = jnp.where(lower_mask, jnp.exp(jnp.where(lower_mask, gaps, 0.0)), 0.0)
        scores = jnp.dot(c_blk, b_blk.T, precision=highest)
        mixing = decay_mask * scores
        output = jnp.einsum('hts,shp->thp', mixing, x_blk, precision=highest)
        output = output + jnp.exp(cumulative).T[:, :, None] * jnp.einsum('hpn,tn->thp', state, c_blk, precision=highest)
        output = output + skip_gain[None, :, None] * x_blk
        tail_decay = jnp.exp(cumulative[:, -1:] - cumulative)
        fresh_state = jnp.einsum('hs,shp,sn->hpn', tail_decay, x_blk, b_blk, precision=highest)
        state = jnp.exp(cumulative[:, -1])[:, None, None] * state + fresh_state
        return (state, output)
    start_state = jnp.zeros((HEAD_GROUP, P_SIZE, N), jnp.float32)
    final_state, outputs = lax.scan(jax.checkpoint(advance), start_state, (x_blocks, d_blocks, b_blocks, c_blocks))
    return outputs.reshape(TOKEN_WINDOW, HEAD_GROUP * P_SIZE)

def adapter(hidden, down_weight, up_weight, block_lang):
    lang_tok = jnp.repeat(block_lang, BLK)
    one_hot = (lang_tok[:, None] == jnp.arange(LANG, dtype=jnp.int32)[None, :]).astype(jnp.float32)
    pre_all = jnp.einsum('tf,kfr->tkr', hidden, down_weight, precision=highest)
    pre_act = jnp.einsum('tk,tkr->tr', one_hot, pre_all, precision=highest)
    active = jax.nn.silu(pre_act)
    spread = one_hot[:, :, None] * active[:, None, :]
    return hidden + jnp.einsum('tkr,krf->tf', spread, up_weight, precision=highest)

def reference(seq_input, log_decay, b_proj, c_proj, skip_gain, down_weight, up_weight, block_lang, cotangent):

    def forward(seq_in, b_in, c_in, w_down, w_up):
        hidden = group_free_scan(seq_in, log_decay, b_in, c_in, skip_gain)
        return adapter(hidden, w_down, w_up, block_lang)
    layer_out, pullback = jax.vjp(forward, seq_input, b_proj, c_proj, down_weight, up_weight)
    grads = pullback(cotangent)
    return (layer_out, grads[0], grads[1], grads[2], grads[3], grads[4])
```

```python
import functools

import jax
import jax.numpy as jnp
from jax import lax
from jax.experimental import pallas as pl
from jax.experimental.pallas import tpu as pltpu
from jax.sharding import PartitionSpec as P

P_SIZE = 64
R = 256
LANG = 2
NY = 8
NZ = 8
NMOD = 8
f32 = jnp.float32
MESH = pl.DeviceIdType.MESH
high = lax.Precision.HIGH
VM = pl.BlockSpec(memory_space=pltpu.VMEM)
DMA = pltpu.SemaphoreType.DMA


def rcopy(src, dst, ss, rs, dev):
    return pltpu.make_async_remote_copy(
        src_ref=src, dst_ref=dst, send_sem=ss, recv_sem=rs, device_id=dev, device_id_type=MESH
    )


def ctx_place():
    c = lax.axis_index("ctx")
    return c // NY, c % NY


def y_dev(z, y, d):
    return {"ctx": z * NY + (y + d) % NY}


def z_dev(z, y, d):
    return {"ctx": ((z + d) % NZ) * NY + y}


def meet_ctx(z, y):
    barrier = pltpu.get_barrier_semaphore()
    for d in range(1, NY):
        pl.semaphore_signal(barrier, inc=1, device_id=y_dev(z, y, d), device_id_type=MESH)
    for d in range(1, NZ):
        pl.semaphore_signal(barrier, inc=1, device_id=z_dev(z, y, d), device_id_type=MESH)
    pl.semaphore_wait(barrier, NY + NZ - 2)


def scan_kernel(
    reverse, st_ref, aux_ref, out_ref, auxy_ref,
    gat, gaux, pre, pdec, tot, zg, ret, retin,
    s1, r1, s2, r2, s3, r3, s4, r4,
):
    z, y = ctx_place()
    meet_ctx(z, y)
    first = []
    for d in range(1, NY):
        peer = (y + d) % NY
        a = rcopy(aux_ref.at[peer], gaux.at[d], s2.at[d], r2.at[d], y_dev(z, y, d))
        b = rcopy(st_ref.at[peer], gat.at[d], s1.at[d], r1.at[d], y_dev(z, y, d))
        a.start()
        b.start()
        first += [a, b]
    gat[0] = st_ref[y]
    gaux[0] = aux_ref[y]
    for cp in first:
        cp.wait_recv()
    state = jnp.zeros((P_SIZE, 128), f32)
    dec = jnp.ones((1, 128), f32)
    order = range(NY - 1, -1, -1) if reverse else range(NY)
    for s in order:
        slot = (y - s + NY) % NY
        pre[s] = state
        pdec[s] = jnp.broadcast_to(dec, (8, 128))
        dd = gaux[slot][0:1]
        state = dd * state + gat[slot]
        dec = dd * dec
    tot[0:P_SIZE] = state
    tot[P_SIZE:] = jnp.broadcast_to(dec, (8, 128))
    second = []
    for d in range(1, NZ):
        cp = rcopy(tot, zg.at[d], s3.at[d], r3.at[d], z_dev(z, y, d))
        cp.start()
        second.append(cp)
    auxy_ref[...] = gaux[...]
    zg[0] = tot[...]
    for cp in second:
        cp.wait_recv()
    carry = jnp.zeros((P_SIZE, 128), f32)
    for s in (range(NZ - 1, -1, -1) if reverse else range(NZ)):
        blk = zg[(z - s + NZ) % NZ]
        nxt = blk[P_SIZE : P_SIZE + 1] * carry + blk[0:P_SIZE]
        use = (z < s) if reverse else (z > s)
        carry = jnp.where(use, nxt, carry)
    third = []
    for d in range(1, NY):
        s = (y + d) % NY
        ret[d] = pre[s] + pdec[s][0:1] * carry
        cp = rcopy(ret.at[d], retin.at[d], s4.at[d], r4.at[d], y_dev(z, y, d))
        cp.start()
        third.append(cp)
    retin[0] = pre[y] + pdec[y][0:1] * carry
    for cp in third:
        cp.wait_recv()
    for h in range(NY):
        out_ref[h] = retin[(y - h + NY) % NY]
    for cp in first + second + third:
        cp.wait_send()


def scan_call(state, aux, reverse, cid):
    return pl.pallas_call(
        functools.partial(scan_kernel, reverse),
        name="carry_rev" if reverse else "carry_fwd",
        out_shape=(
            jax.ShapeDtypeStruct((NY, P_SIZE, 128), f32),
            jax.ShapeDtypeStruct((NY, 8, 128), f32),
        ),
        in_specs=[VM, VM],
        out_specs=(VM, VM),
        scratch_shapes=[
            pltpu.VMEM((NY, P_SIZE, 128), f32),
            pltpu.VMEM((NY, 8, 128), f32),
            pltpu.VMEM((NY, P_SIZE, 128), f32),
            pltpu.VMEM((NY, 8, 128), f32),
            pltpu.VMEM((P_SIZE + 8, 128), f32),
            pltpu.VMEM((NZ, P_SIZE + 8, 128), f32),
            pltpu.VMEM((NY, P_SIZE, 128), f32),
            pltpu.VMEM((NY, P_SIZE, 128), f32),
        ]
        + [DMA((8,))] * 8,
        compiler_params=pltpu.CompilerParams(collective_id=cid, has_side_effects=True),
    )(state, aux)


def sum_kernel(x_ref, out_ref, buf, acc, ag, s1, r1, s2, r2):
    m = lax.axis_index("mod")
    barrier = pltpu.get_barrier_semaphore()
    for d in range(1, NMOD):
        pl.semaphore_signal(
            barrier, inc=1, device_id={"mod": (m + d) % NMOD}, device_id_type=MESH
        )
    pl.semaphore_wait(barrier, NMOD - 1)
    first, second = [], []
    for d in range(1, NMOD):
        peer = (m + d) % NMOD
        cp = rcopy(x_ref.at[peer], buf.at[d], s1.at[d], r1.at[d], {"mod": peer})
        cp.start()
        first.append(cp)
    total = x_ref[m]
    for d in range(1, NMOD):
        first[d - 1].wait_recv()
        total = total + buf[d]
    acc[...] = total
    for d in range(1, NMOD):
        cp = rcopy(acc, ag.at[d], s2.at[d], r2.at[d], {"mod": (m + d) % NMOD})
        cp.start()
        second.append(cp)
    ag[0] = total
    for cp in second:
        cp.wait_recv()
    for h in range(NMOD):
        out_ref[h] = ag[(m - h + NMOD) % NMOD]
    for cp in first + second:
        cp.wait_send()


def sum_call(x, cid):
    rows, cols = x.shape
    part = (NMOD, rows // NMOD, cols)
    out = pl.pallas_call(
        sum_kernel,
        name="sum_mod_%d" % cid,
        out_shape=jax.ShapeDtypeStruct(part, f32),
        in_specs=[VM],
        out_specs=VM,
        scratch_shapes=[pltpu.VMEM(part, f32), pltpu.VMEM(part[1:], f32), pltpu.VMEM(part, f32)]
        + [DMA((8,))] * 4,
        compiler_params=pltpu.CompilerParams(collective_id=cid, has_side_effects=True),
    )(x.reshape(part))
    return out.reshape(rows, cols)


def grad_kernel(g_ref, lang_ref, out_ref, buf, part, zbuf, s1, r1, s2, r2):
    z, y = ctx_place()
    meet_ctx(z, y)
    first, second = [], []
    for d in range(1, NY):
        cp = rcopy(g_ref.at[(y + d) % NY], buf.at[d], s1.at[d], r1.at[d], y_dev(z, y, d))
        cp.start()
        first.append(cp)
    buf[0] = g_ref[y]
    for cp in first:
        cp.wait_recv()

    @pl.loop(0, NZ)
    def _(t):
        zero = jnp.zeros((8, 512), f32)
        a, b = zero, zero
        for d in range(NY):
            v = buf[d, t]
            w = jnp.broadcast_to(lang_ref[d][1:2, 0:1], (8, 512))
            a = a + jnp.where(w < 0.5, v, 0.0)
            b = b + jnp.where(w < 0.5, 0.0, v)
        part[t, 0] = a
        part[t, 1] = b

    for d in range(1, NZ):
        cp = rcopy(part.at[(z + d) % NZ], zbuf.at[d], s2.at[d], r2.at[d], z_dev(z, y, d))
        cp.start()
        second.append(cp)
    total = part[z]
    for d in range(1, NZ):
        second[d - 1].wait_recv()
        total = total + zbuf[d]
    out_ref[...] = total
    for cp in first + second:
        cp.wait_send()


def grad_call(g, lang, cid):
    return pl.pallas_call(
        grad_kernel,
        name="weight_grads",
        out_shape=jax.ShapeDtypeStruct((LANG, 8, 512), f32),
        in_specs=[VM, VM],
        out_specs=VM,
        scratch_shapes=[
            pltpu.VMEM((NY, NZ, 8, 512), f32),
            pltpu.VMEM((NZ, LANG, 8, 512), f32),
            pltpu.VMEM((NZ, LANG, 8, 512), f32),
        ]
        + [DMA((8,))] * 4,
        compiler_params=pltpu.CompilerParams(collective_id=cid, has_side_effects=True),
    )(g, lang)


def ein(spec, *args):
    return jnp.einsum(spec, *args, precision=high)


def shards(
    seq_input, log_decay, b_proj, c_proj, skip_gain, down_weight, up_weight, block_lang, cotangent
):
    rows, width = seq_input.shape
    heads = log_decay.shape[0]
    x = seq_input.reshape(rows, heads, P_SIZE)
    cumulative = jnp.cumsum(log_decay, axis=1)
    lower = jnp.tril(jnp.ones((rows, rows), bool))
    gaps = cumulative[:, :, None] - cumulative[:, None, :]
    decay_mask = jnp.where(lower, jnp.exp(jnp.where(lower, gaps, 0.0)), 0.0)
    mixing = decay_mask * ein("tn,sn->ts", c_proj, b_proj)
    tail = jnp.exp(cumulative[:, -1:] - cumulative)
    total = jnp.exp(cumulative[:, -1])
    head = jnp.exp(cumulative)
    lang = block_lang[0]
    down = lax.dynamic_index_in_dim(down_weight, lang, 0, False)
    up = lax.dynamic_index_in_dim(up_weight, lang, 0, False)

    aux = jnp.where(
        jnp.arange(8)[None, :, None] == 0, total[:, None, None], lang.astype(f32)
    ) + jnp.zeros((heads, 8, 128), f32)
    local_state = ein("shp,sn->hpn", tail.T[:, :, None] * x, b_proj)
    state_in, aux_y = scan_call(local_state, aux, False, 1)
    hidden = ein("hts,shp->thp", mixing, x)
    hidden = hidden + skip_gain[None, :, None] * x
    hidden = hidden + head.T[:, :, None] * ein("hpn,tn->thp", state_in, c_proj)
    hidden = hidden.reshape(rows, width)
    pre_part = ein("tf,fr->tr", hidden, down)
    back_part = ein("tf,rf->tr", cotangent, up)
    both = sum_call(jnp.concatenate([pre_part, back_part], axis=1), 2)
    pre_act, back_act = both[:, :R], both[:, R:]
    gate = jax.nn.sigmoid(pre_act)
    active = pre_act * gate
    pre_grad = back_act * (gate * (1.0 + pre_act * (1.0 - gate)))
    hidden_grad = cotangent + ein("tr,fr->tf", pre_grad, down)
    gh = hidden_grad.reshape(rows, heads, P_SIZE)
    local_adjoint = ein("shp,sn->hpn", head.T[:, :, None] * gh, c_proj)
    adjoint_in, _ = scan_call(local_adjoint, aux, True, 3)

    layer_out = hidden + ein("tr,rf->tf", active, up)
    down_t = ein("tr,tf->rf", pre_grad, hidden).reshape(NZ, NY, 4, width)
    up_t = ein("tr,tf->rf", active, cotangent).reshape(NZ, NY, 4, width)
    g = jnp.concatenate([down_t, up_t], axis=2).transpose(1, 0, 2, 3)
    wg = grad_call(g, aux_y, 4)
    down_grad = wg[:, :4].transpose(0, 2, 1)
    up_grad = wg[:, 4:]

    input_grad = ein("hts,thp->shp", mixing, gh) + skip_gain[None, :, None] * gh
    input_grad = input_grad + tail.T[:, :, None] * ein("hpn,sn->shp", adjoint_in, b_proj)
    weighted = jnp.sum(decay_mask * ein("thp,shp->hts", gh, x), axis=0)
    b_part = ein("ts,tn->sn", weighted, c_proj)
    b_part = b_part + ein("shp,hpn->sn", tail.T[:, :, None] * x, adjoint_in)
    c_part = ein("ts,sn->tn", weighted, b_proj)
    c_part = c_part + ein("thp,hpn->tn", head.T[:, :, None] * gh, state_in)
    bc = sum_call(jnp.concatenate([b_part, c_part], axis=1), 5)
    return (layer_out, input_grad.reshape(rows, width), bc[:, :128], bc[:, 128:], down_grad, up_grad)


def solution(mesh):
    return jax.shard_map(
        shards,
        mesh=mesh,
        in_specs=(
            P("ctx", "mod"),
            P("mod", "ctx"),
            P("ctx", None),
            P("ctx", None),
            P("mod"),
            P(None, "mod", None),
            P(None, None, "mod"),
            P("ctx"),
            P("ctx", "mod"),
        ),
        out_specs=(
            P("ctx", "mod"),
            P("ctx", "mod"),
            P("ctx", None),
            P("ctx", None),
            P(None, "mod", "ctx"),
            P(None, "ctx", "mod"),
        ),
        check_vma=False,
    )
```

```python
import functools

import jax
import jax.numpy as jnp
from jax import lax
from jax.experimental import pallas as pl
from jax.experimental.pallas import tpu as pltpu
from jax.sharding import PartitionSpec as P

P_SIZE = 64
R = 256
LANG = 2
NY = 8
NZ = 8
NMOD = 8
f32 = jnp.float32
MESH = pl.DeviceIdType.MESH
high = lax.Precision.HIGH
VM = pl.BlockSpec(memory_space=pltpu.VMEM)
DMA = pltpu.SemaphoreType.DMA


def rcopy(src, dst, ss, rs, dev):
    return pltpu.make_async_remote_copy(
        src_ref=src, dst_ref=dst, send_sem=ss, recv_sem=rs, device_id=dev, device_id_type=MESH
    )


def ctx_place():
    c = lax.axis_index("ctx")
    return c // NY, c % NY, lax.axis_index("mod")


def y_dev(z, y, d):
    return {"ctx": z * NY + (y + d) % NY}


def z_dev(z, y, d):
    return {"ctx": ((z + d) % NZ) * NY + y}


def m_dev(m, d):
    return {"mod": (m + d) % NMOD}


def meet(z, y, m):
    barrier = pltpu.get_barrier_semaphore()
    for d in range(1, 8):
        for dev in (y_dev(z, y, d), z_dev(z, y, d), m_dev(m, d)):
            pl.semaphore_signal(barrier, inc=1, device_id=dev, device_id_type=MESH)
    pl.semaphore_wait(barrier, 21)


def dot3(a, b, ca, cb):
    def split(v):
        top = v.astype(jnp.bfloat16)
        return top, (v - top.astype(f32)).astype(jnp.bfloat16)

    def one(p, q):
        return lax.dot_general(p, q, (((ca,), (cb,)), ((), ())), preferred_element_type=f32)

    (ah, al), (bh, bl) = split(a), split(b)
    return one(ah, bh) + (one(ah, bl) + one(al, bh))


def send_all(pick, dst, ss, rs, dev):
    out = []
    for d in range(1, 8):
        cp = rcopy(pick(d), dst.at[d], ss.at[d], rs.at[d], dev(d))
        cp.start()
        out.append(cp)
    return out


def arrive(copies):
    for cp in copies:
        cp.wait_recv()


def add_up(own, copies, buf):
    total = own
    for d in range(1, 8):
        copies[d - 1].wait_recv()
        total = total + buf[d]
    return total


def row_prefix(reverse, y, gat, gaux, pre, pdec):
    state = jnp.zeros((P_SIZE, 128), f32)
    dec = jnp.ones((1, 128), f32)
    for s in range(NY - 1, -1, -1) if reverse else range(NY):
        slot = (y - s + NY) % NY
        pre[s] = state
        pdec[s] = jnp.broadcast_to(dec, (8, 128))
        dd = gaux[slot][0:1]
        state = dd * state + gat[slot]
        dec = dd * dec
    return state, dec


def row_carry(reverse, z, state_of, dec_of):
    carry = jnp.zeros((P_SIZE, 128), f32)
    for s in range(NZ - 1, -1, -1) if reverse else range(NZ):
        slot = (z - s + NZ) % NZ
        nxt = dec_of(slot) * carry + state_of(slot)
        use = (z < s) if reverse else (z > s)
        carry = jnp.where(use, nxt, carry)
    return carry


def fwd_kernel(
    st_ref, aux_ref, back_ref, hid_ref, head_ref, c_ref, down_ref,
    state_ref, auxy_ref, auxz_ref, hidden_ref, pre_ref, backsum_ref,
    gat, gaux, pre, pdec, tot, zg, ret, retin, part, rbuf, racc, rag, bbuf, bacc, bag,
    s1, r1, s2, r2, s3, r3, s4, r4, s5, r5, s6, r6, s7, r7, s8, r8,
):
    z, y, m = ctx_place()
    meet(z, y, m)
    ydev = lambda d: y_dev(z, y, d)
    zdev = lambda d: z_dev(z, y, d)
    mdev = lambda d: m_dev(m, d)
    c2 = send_all(lambda d: aux_ref.at[(y + d) % NY], gaux, s2, r2, ydev)
    c1 = send_all(lambda d: st_ref.at[(y + d) % NY], gat, s1, r1, ydev)
    c5 = send_all(lambda d: back_ref.at[(m + d) % NMOD], bbuf, s5, r5, mdev)
    gat[0] = st_ref[y]
    gaux[0] = aux_ref[y]
    arrive(c2 + c1)
    state, dec = row_prefix(False, y, gat, gaux, pre, pdec)
    tot[0:P_SIZE] = state
    lang_row = aux_ref[0][1:2]
    tot[P_SIZE:] = jnp.where(
        lax.broadcasted_iota(jnp.int32, (8, 128), 0) == 0,
        jnp.broadcast_to(dec, (8, 128)),
        jnp.broadcast_to(lang_row, (8, 128)),
    )
    c3 = send_all(lambda d: tot, zg, s3, r3, zdev)
    bacc[...] = add_up(back_ref[m], c5, bbuf)
    c6 = send_all(lambda d: bacc, bag, s6, r6, mdev)
    auxy_ref[...] = gaux[...]
    zg[0] = tot[...]
    arrive(c3)
    carry = row_carry(
        False, z, lambda i: zg[i, 0:P_SIZE], lambda i: zg[i, P_SIZE : P_SIZE + 8][0:1]
    )
    c4 = []
    for d in range(1, NY):
        s = (y + d) % NY
        ret[d] = pre[s] + pdec[s][0:1] * carry
        cp = rcopy(ret.at[d], retin.at[d], s4.at[d], r4.at[d], ydev(d))
        cp.start()
        c4.append(cp)
    retin[0] = pre[y] + pdec[y][0:1] * carry
    for d in range(NZ):
        auxz_ref[d] = zg[d, P_SIZE:]
    bag[0] = bacc[...]
    arrive(c6)
    for h in range(NMOD):
        backsum_ref[h] = bag[(m - h + NMOD) % NMOD]
    arrive(c4)
    for h in range(NY):
        state_ref[h] = retin[(y - h + NY) % NY]
    flat = state_ref[...].reshape(NY * P_SIZE, 128)
    hidden = hid_ref[...] + head_ref[...] * dot3(c_ref[...], flat, 1, 1)
    hidden_ref[...] = hidden
    part[...] = dot3(hidden, down_ref[...], 1, 0).reshape(NMOD, 16, R)
    c7 = send_all(lambda d: part.at[(m + d) % NMOD], rbuf, s7, r7, mdev)
    racc[...] = add_up(part[m], c7, rbuf)
    c8 = send_all(lambda d: racc, rag, s8, r8, mdev)
    rag[0] = racc[...]
    arrive(c8)
    for h in range(NMOD):
        pre_ref[h] = rag[(m - h + NMOD) % NMOD]
    for cp in c1 + c2 + c3 + c4 + c5 + c6 + c7 + c8:
        cp.wait_send()


def by_lang(buf, aux, out):
    def body(t, _):
        a, b = jnp.zeros((8, 256), f32), jnp.zeros((8, 256), f32)
        for d in range(8):
            v = buf[d, t]
            first = jnp.broadcast_to(aux[d][1:2, 0:1], (8, 256)) < 0.5
            a = a + jnp.where(first, v, 0.0)
            b = b + jnp.where(first, 0.0, v)
        out[t, 0] = a
        out[t, 1] = b
        return 0

    lax.fori_loop(0, 8, body, 0)


def bwd_kernel(
    st_ref, auxy_ref, auxz_ref, ga_ref, gb_ref, xt_ref, b_ref, c_ref,
    adj_ref, wa_ref, wb_ref, bsum_ref, csum_ref,
    gat, pre, pdec, tot, zg, ret, retin,
    abuf, apart, azbuf, zbuf, zpart, zybuf,
    cbuf, cacc, cag, part, rbuf, racc, rag,
    s1, r1, s3, r3, s4, r4, s5, r5, s6, r6, s7, r7, s8, r8,
    sa, ra, sb, rb, sc, rc, sd, rd, se, re, sf, rf,
):
    z, y, m = ctx_place()
    meet(z, y, m)
    ydev = lambda d: y_dev(z, y, d)
    zdev = lambda d: z_dev(z, y, d)
    mdev = lambda d: m_dev(m, d)

    def send_half(src, dst, place, half, ss, rs, dev):
        out = []
        for d in range(1, 8):
            cp = rcopy(
                src.at[(place + d) % 8, pl.ds(4 * half, 4)],
                dst.at[d, pl.ds(4 * half, 4)],
                ss.at[d], rs.at[d], dev(d),
            )
            cp.start()
            out.append(cp)
        return out

    c1 = send_all(lambda d: st_ref.at[(y + d) % NY], gat, s1, r1, ydev)
    c5 = send_all(lambda d: c_ref.at[(m + d) % NMOD], cbuf, s5, r5, mdev)
    cb0 = send_half(gb_ref, zbuf, z, 0, sc, rc, zdev)
    gat[0] = st_ref[y]
    arrive(c1)
    state, dec = row_prefix(True, y, gat, auxy_ref, pre, pdec)
    tot[...] = state
    c3 = send_all(lambda d: tot, zg, s3, r3, zdev)
    cb1 = send_half(gb_ref, zbuf, z, 1, sd, rd, zdev)
    ca0 = send_half(ga_ref, abuf, y, 0, sa, ra, ydev)
    cacc[...] = add_up(c_ref[m], c5, cbuf)
    c6 = send_all(lambda d: cacc, cag, s6, r6, mdev)
    zg[0] = tot[...]
    arrive(c3)
    carry = row_carry(True, z, lambda i: zg[i], lambda i: auxz_ref[i][0:1])
    c4 = []
    for d in range(1, NY):
        s = (y + d) % NY
        ret[d] = pre[s] + pdec[s][0:1] * carry
        cp = rcopy(ret.at[d], retin.at[d], s4.at[d], r4.at[d], ydev(d))
        cp.start()
        c4.append(cp)
    ca1 = send_half(ga_ref, abuf, y, 1, sb, rb, ydev)
    retin[0] = pre[y] + pdec[y][0:1] * carry
    abuf[0] = ga_ref[y]
    zbuf[0] = gb_ref[z]
    cag[0] = cacc[...]
    arrive(c6)
    for h in range(NMOD):
        csum_ref[h] = cag[(m - h + NMOD) % NMOD]
    arrive(c4)
    for h in range(NY):
        adj_ref[h] = retin[(y - h + NY) % NY]
    flat = adj_ref[...].reshape(NY * P_SIZE, 128)
    part[...] = (b_ref[...] + dot3(xt_ref[...], flat, 1, 0)).reshape(NMOD, 16, 128)
    c7 = send_all(lambda d: part.at[(m + d) % NMOD], rbuf, s7, r7, mdev)
    arrive(cb0 + cb1)
    by_lang(zbuf, auxz_ref, zpart)
    ce = send_all(lambda d: zpart.at[(y + d) % NY], zybuf, se, re, ydev)
    racc[...] = add_up(part[m], c7, rbuf)
    c8 = send_all(lambda d: racc, rag, s8, r8, mdev)
    arrive(ca0 + ca1)
    by_lang(abuf, auxy_ref, apart)
    cf = send_all(lambda d: apart.at[(z + d) % NZ], azbuf, sf, rf, zdev)
    rag[0] = racc[...]
    arrive(c8)
    for h in range(NMOD):
        bsum_ref[h] = rag[(m - h + NMOD) % NMOD]
    wb_ref[...] = add_up(zpart[y], ce, zybuf)
    wa_ref[...] = add_up(apart[z], cf, azbuf)
    for cp in c1 + c3 + c4 + c5 + c6 + c7 + c8 + ca0 + ca1 + cb0 + cb1 + ce + cf:
        cp.wait_send()


def vmem(*shape):
    return pltpu.VMEM(shape, f32)


def out_of(*shape):
    return jax.ShapeDtypeStruct(shape, f32)


def fwd_call(*args):
    chunk = (NMOD, 16, R)
    return pl.pallas_call(
        fwd_kernel,
        name="forward",
        out_shape=(
            out_of(8, P_SIZE, 128), out_of(8, 8, 128), out_of(8, 8, 128), out_of(128, 512),
            out_of(*chunk), out_of(*chunk),
        ),
        in_specs=[VM] * 7,
        out_specs=(VM,) * 6,
        scratch_shapes=[
            vmem(8, P_SIZE, 128), vmem(8, 8, 128), vmem(8, P_SIZE, 128), vmem(8, 8, 128),
            vmem(P_SIZE + 8, 128), vmem(8, P_SIZE + 8, 128),
            vmem(8, P_SIZE, 128), vmem(8, P_SIZE, 128),
            vmem(*chunk), vmem(*chunk), vmem(16, R), vmem(*chunk),
            vmem(*chunk), vmem(16, R), vmem(*chunk),
        ]
        + [DMA((8,))] * 16,
        compiler_params=pltpu.CompilerParams(collective_id=1, has_side_effects=True),
    )(*args)


def bwd_call(*args):
    chunk = (NMOD, 16, 128)
    big = (8, 8, 8, 256)
    mid = (8, LANG, 8, 256)
    return pl.pallas_call(
        bwd_kernel,
        name="backward",
        out_shape=(
            out_of(8, P_SIZE, 128), out_of(*mid[1:]), out_of(*mid[1:]), out_of(*chunk),
            out_of(*chunk),
        ),
        in_specs=[VM] * 8,
        out_specs=(VM,) * 5,
        scratch_shapes=[
            vmem(8, P_SIZE, 128), vmem(8, P_SIZE, 128), vmem(8, 8, 128),
            vmem(P_SIZE, 128), vmem(8, P_SIZE, 128),
            vmem(8, P_SIZE, 128), vmem(8, P_SIZE, 128),
            vmem(*big), vmem(*mid), vmem(*mid), vmem(*big), vmem(*mid), vmem(*mid),
            vmem(*chunk), vmem(16, 128), vmem(*chunk),
            vmem(*chunk), vmem(*chunk), vmem(16, 128), vmem(*chunk),
        ]
        + [DMA((8,))] * 26,
        compiler_params=pltpu.CompilerParams(collective_id=2, has_side_effects=True),
    )(*args)


def ein(spec, *args):
    return jnp.einsum(spec, *args, precision=high)


def shards(
    seq_input, log_decay, b_proj, c_proj, skip_gain, down_weight, up_weight, block_lang, cotangent
):
    rows, width = seq_input.shape
    heads = log_decay.shape[0]
    x = seq_input.reshape(rows, heads, P_SIZE)
    cumulative = jnp.cumsum(log_decay, axis=1)
    lower = jnp.tril(jnp.ones((rows, rows), bool))
    gaps = cumulative[:, :, None] - cumulative[:, None, :]
    decay_mask = jnp.where(lower, jnp.exp(jnp.where(lower, gaps, 0.0)), 0.0)
    mixing = decay_mask * ein("tn,sn->ts", c_proj, b_proj)
    tail = jnp.exp(cumulative[:, -1:] - cumulative)
    total = jnp.exp(cumulative[:, -1])
    head = jnp.exp(cumulative)
    lang = block_lang[0]
    down = lax.dynamic_index_in_dim(down_weight, lang, 0, False)
    up = lax.dynamic_index_in_dim(up_weight, lang, 0, False)

    aux = jnp.where(
        jnp.arange(8)[None, :, None] == 0, total[:, None, None], lang.astype(f32)
    ) + jnp.zeros((heads, 8, 128), f32)
    local_state = ein("shp,sn->hpn", tail.T[:, :, None] * x, b_proj)
    head_full = jnp.repeat(head.T, P_SIZE, axis=1)
    back_part = ein("tf,rf->tr", cotangent, up)
    hid = ein("hts,shp->thp", mixing, x) + skip_gain[None, :, None] * x
    chunk = (NMOD, rows // NMOD, -1)
    state_in, aux_y, aux_z, hidden, pre_sum, back_sum = fwd_call(
        local_state, aux, back_part.reshape(chunk), hid.reshape(rows, width), head_full,
        c_proj, down,
    )
    pre_act, back_act = pre_sum.reshape(rows, R), back_sum.reshape(rows, R)
    gate = jax.nn.sigmoid(pre_act)
    active = pre_act * gate
    pre_grad = back_act * (gate * (1.0 + pre_act * (1.0 - gate)))
    hidden_grad = cotangent + ein("tr,fr->tf", pre_grad, down)
    gh = hidden_grad.reshape(rows, heads, P_SIZE)
    local_adjoint = ein("shp,sn->hpn", head.T[:, :, None] * gh, c_proj)
    layer_out = hidden + ein("tr,rf->tf", active, up)
    down_t = ein("tr,tf->rf", pre_grad, hidden).reshape(NZ, NY, 4, width)
    up_t = ein("tr,tf->rf", active, cotangent).reshape(NZ, NY, 4, width)
    g = jnp.concatenate([down_t, up_t], axis=2)
    half = width // 2
    weighted = jnp.sum(decay_mask * ein("thp,shp->hts", gh, x), axis=0)
    b_part = ein("ts,tn->sn", weighted, c_proj)
    c_part = ein("ts,sn->tn", weighted, b_proj)
    c_part = c_part + ein("thp,hpn->tn", head.T[:, :, None] * gh, state_in)
    xt = (tail.T[:, :, None] * x).reshape(rows, width)
    adjoint_in, wa, wb, b_sum, c_sum = bwd_call(
        local_adjoint, aux_y, aux_z, g[..., :half].transpose(1, 0, 2, 3), g[..., half:],
        xt, b_part, c_part.reshape(chunk),
    )
    wg = jnp.concatenate([wa, wb], axis=2)
    input_grad = ein("hts,thp->shp", mixing, gh) + skip_gain[None, :, None] * gh
    input_grad = input_grad + tail.T[:, :, None] * ein("hpn,sn->shp", adjoint_in, b_proj)
    return (
        layer_out,
        input_grad.reshape(rows, width),
        b_sum.reshape(rows, 128),
        c_sum.reshape(rows, 128),
        wg[:, :4].transpose(0, 2, 1),
        wg[:, 4:],
    )


def solution(mesh):
    return jax.shard_map(
        shards,
        mesh=mesh,
        in_specs=(
            P("ctx", "mod"),
            P("mod", "ctx"),
            P("ctx", None),
            P("ctx", None),
            P("mod"),
            P(None, "mod", None),
            P(None, None, "mod"),
            P("ctx"),
            P("ctx", "mod"),
        ),
        out_specs=(
            P("ctx", "mod"),
            P("ctx", "mod"),
            P("ctx", None),
            P("ctx", None),
            P(None, "mod", "ctx"),
            P(None, "ctx", "mod"),
        ),
        check_vma=False,
    )
```

```python
import jax
import jax.numpy as jnp
from jax import lax
from jax.experimental import pallas as pl
from jax.experimental.pallas import tpu as pltpu
from jax.sharding import PartitionSpec as P

P_SIZE = 64
R = 256
LANG = 2
NY = 8
NZ = 8
NMOD = 8
f32 = jnp.float32
MESH = pl.DeviceIdType.MESH
VM = pl.BlockSpec(memory_space=pltpu.VMEM)
DMA = pltpu.SemaphoreType.DMA


def rcopy(src, dst, ss, rs, dev):
    return pltpu.make_async_remote_copy(
        src_ref=src, dst_ref=dst, send_sem=ss, recv_sem=rs, device_id=dev, device_id_type=MESH
    )


def ctx_place():
    c = lax.axis_index("ctx")
    return c // NY, c % NY, lax.axis_index("mod")


def y_dev(z, y, d):
    return {"ctx": z * NY + (y + d) % NY}


def z_dev(z, y, d):
    return {"ctx": ((z + d) % NZ) * NY + y}


def m_dev(m, d):
    return {"mod": (m + d) % NMOD}


def greet(z, y, m):
    barrier = pltpu.get_barrier_semaphore()
    for d in range(1, 8):
        for dev in (y_dev(z, y, d), z_dev(z, y, d), m_dev(m, d)):
            pl.semaphore_signal(barrier, inc=1, device_id=dev, device_id_type=MESH)


def dot3(a, b, ca, cb):
    def split(v):
        top = v.astype(jnp.bfloat16)
        return top, (v - top.astype(f32)).astype(jnp.bfloat16)

    def one(p, q):
        return lax.dot_general(p, q, (((ca,), (cb,)), ((), ())), preferred_element_type=f32)

    (ah, al), (bh, bl) = split(a), split(b)
    return one(ah, bh) + (one(ah, bl) + one(al, bh))


def send_all(pick, dst, ss, rs, dev):
    out = []
    for d in range(1, 8):
        cp = rcopy(pick(d), dst.at[d], ss.at[d], rs.at[d], dev(d))
        cp.start()
        out.append(cp)
    return out


def arrive(copies):
    for cp in copies:
        cp.wait_recv()


def add_up(own, copies, buf):
    total = own
    for d in range(1, 8):
        copies[d - 1].wait_recv()
        total = total + buf[d]
    return total


def row_prefix(reverse, y, gat, gaux, pre, pdec):
    state = jnp.zeros((P_SIZE, 128), f32)
    dec = jnp.ones((1, 128), f32)
    for s in range(NY - 1, -1, -1) if reverse else range(NY):
        slot = (y - s + NY) % NY
        pre[s] = state
        pdec[s] = jnp.broadcast_to(dec, (8, 128))
        dd = gaux[slot][0:1]
        state = dd * state + gat[slot]
        dec = dd * dec
    return state, dec


def row_carry(reverse, z, state_of, dec_of):
    carry = jnp.zeros((P_SIZE, 128), f32)
    for s in range(NZ - 1, -1, -1) if reverse else range(NZ):
        slot = (z - s + NZ) % NZ
        nxt = dec_of(slot) * carry + state_of(slot)
        use = (z < s) if reverse else (z > s)
        carry = jnp.where(use, nxt, carry)
    return carry


def by_lang(buf, aux, out):
    def body(t, _):
        a, b = jnp.zeros((8, 256), f32), jnp.zeros((8, 256), f32)
        for d in range(8):
            v = buf[d, t]
            first = jnp.broadcast_to(aux[d][1:2, 0:1], (8, 256)) < 0.5
            a = a + jnp.where(first, v, 0.0)
            b = b + jnp.where(first, 0.0, v)
        out[t, 0] = a
        out[t, 1] = b
        return 0

    lax.fori_loop(0, 8, body, 0)


def layer_kernel(
    lang_ref, x_ref, ld_ref, b_ref, c_ref, skip_ref, down_ref, up_ref, cot_ref,
    out_ref, ig_ref, bsum_ref, csum_ref, downg_ref, upg_ref,
    st, aux, gat, gaux, pre, pdec, tot, zg, ret, retin,
    back, bbuf, bacc, bag, part, rbuf, racc, rag,
    st2, gat2, tot2, zg2, ret2, retin2,
    g, abuf, apart, azbuf, zbuf, zpart, zybuf, auxz,
    cpart, cbuf, cacc, cag, bpart, xbuf, xacc, xag,
    mix, dmask, hid, headf, tailf, ghs, wg,
    s1, r1, s2, r2, s3, r3, s4, r4, s5, r5, s6, r6, s7, r7, s8, r8,
    t1, q1, t3, q3, t4, q4, t5, q5, t6, q6, t7, q7, t8, q8,
    sa, ra, sb, rb, sc, rc, sd, rd, se, re, sf, rf,
):
    z, y, m = ctx_place()
    greet(z, y, m)
    ydev = lambda d: y_dev(z, y, d)
    zdev = lambda d: z_dev(z, y, d)
    mdev = lambda d: m_dev(m, d)
    lang = lang_ref[0]
    iota = lambda shape, dim: lax.broadcasted_iota(jnp.int32, shape, dim)
    sq = (128, 128)
    lower = iota(sq, 0) >= iota(sq, 1)
    left = iota(sq, 1) < P_SIZE
    pairs = [slice(128 * p, 128 * p + 128) for p in range(4)]

    def spread(v, p):
        return jnp.where(
            left,
            jnp.broadcast_to(v[:, 2 * p : 2 * p + 1], sq),
            jnp.broadcast_to(v[:, 2 * p + 1 : 2 * p + 2], sq),
        )

    ones = lower.astype(f32)
    ld = ld_ref[...]
    full = lax.Precision.HIGHEST
    cum_row = lax.dot_general(
        ld, ones, (((1,), (1,)), ((), ())), precision=full, preferred_element_type=f32
    )
    cum_col = lax.dot_general(
        ones, ld, (((1,), (1,)), ((), ())), precision=full, preferred_element_type=f32
    )
    tail_c = jnp.exp(cum_col[127:128, :] - cum_col)
    head_c = jnp.exp(cum_col)
    for p in range(4):
        tailf[:, pairs[p]] = spread(tail_c, p)
        headf[:, pairs[p]] = spread(head_c, p)
    b, c = b_ref[...], c_ref[...]
    st[...] = dot3(tailf[...] * x_ref[...], b, 0, 0).reshape(8, P_SIZE, 128)
    total = jnp.exp(cum_row[:, 127:128])
    lang_tile = jnp.full((8, 128), lang.astype(f32), f32)
    top_row = iota((8, 128), 0) == 0
    for h in range(8):
        aux[h] = jnp.where(top_row, jnp.broadcast_to(total[h : h + 1, :], (8, 128)), lang_tile)
    pl.semaphore_wait(pltpu.get_barrier_semaphore(), 21)

    c2 = send_all(lambda d: aux.at[(y + d) % NY], gaux, s2, r2, ydev)
    c1 = send_all(lambda d: st.at[(y + d) % NY], gat, s1, r1, ydev)
    gat[0] = st[y]
    gaux[0] = aux[y]
    back[...] = dot3(cot_ref[...], up_ref[lang], 1, 1).reshape(NMOD, 16, R)
    c5 = send_all(lambda d: back.at[(m + d) % NMOD], bbuf, s5, r5, mdev)
    scores = dot3(c, b, 1, 1)
    for p in range(4):
        xp = x_ref[:, pairs[p]]
        got = []
        for h in (2 * p, 2 * p + 1):
            gap = jnp.broadcast_to(cum_col[:, h : h + 1], sq) - jnp.broadcast_to(
                cum_row[h : h + 1, :], sq
            )
            dm = jnp.where(lower, jnp.exp(jnp.where(lower, gap, 0.0)), 0.0)
            dmask[h] = dm
            mix[h] = dm * scores
            got.append(dot3(mix[h], xp, 1, 0))
        hid[:, pairs[p]] = jnp.where(left, got[0], got[1]) + skip_ref[:, pairs[p]] * xp
    arrive(c2 + c1)
    state, dec = row_prefix(False, y, gat, gaux, pre, pdec)
    tot[0:P_SIZE] = state
    tot[P_SIZE:] = jnp.where(top_row, jnp.broadcast_to(dec, (8, 128)), lang_tile)
    c3 = send_all(lambda d: tot, zg, s3, r3, zdev)
    bacc[...] = add_up(back[m], c5, bbuf)
    c6 = send_all(lambda d: bacc, bag, s6, r6, mdev)
    zg[0] = tot[...]
    bag[0] = bacc[...]
    arrive(c3)
    carry = row_carry(
        False, z, lambda i: zg[i, 0:P_SIZE], lambda i: zg[i, P_SIZE : P_SIZE + 8][0:1]
    )

    def send_back(pre, carry, ret, retin, ss, rs):
        out = []
        for d in range(1, NY):
            s = (y + d) % NY
            ret[d] = pre[s] + pdec[s][0:1] * carry
            cp = rcopy(ret.at[d], retin.at[d], ss.at[d], rs.at[d], ydev(d))
            cp.start()
            out.append(cp)
        retin[0] = pre[y] + pdec[y][0:1] * carry
        return out

    def in_order(buf, place):
        return jnp.concatenate([buf[(place - h + 8) % 8] for h in range(8)], axis=0)

    c4 = send_back(pre, carry, ret, retin, s4, r4)
    for d in range(NZ):
        auxz[d] = zg[d, P_SIZE:]
    arrive(c6)
    back_act = in_order(bag, m)
    arrive(c4)
    state_in = in_order(retin, y)
    hid[...] = hid[...] + headf[...] * dot3(c, state_in, 1, 1)
    part[...] = dot3(hid[...], down_ref[lang], 1, 0).reshape(NMOD, 16, R)
    c7 = send_all(lambda d: part.at[(m + d) % NMOD], rbuf, s7, r7, mdev)
    racc[...] = add_up(part[m], c7, rbuf)
    c8 = send_all(lambda d: racc, rag, s8, r8, mdev)
    rag[0] = racc[...]
    arrive(c8)
    pre_act = in_order(rag, m)
    gate = jax.nn.sigmoid(pre_act)
    active = pre_act * gate
    pre_grad = back_act * (gate * (1.0 + pre_act * (1.0 - gate)))

    gh = cot_ref[...] + dot3(pre_grad, down_ref[lang], 1, 1)
    ghs[...] = gh
    head_gh = headf[...] * gh
    st2[...] = dot3(head_gh, c, 0, 0).reshape(8, P_SIZE, 128)
    e1 = send_all(lambda d: st2.at[(y + d) % NY], gat2, t1, q1, ydev)
    gat2[0] = st2[y]

    col = iota((R, 2 * R), 1)
    pick = (iota((R, 2 * R), 0) == 4 * (col // 8) + col % 4).astype(f32)
    both = jnp.where(
        iota((128, 2 * R), 1) % 8 < 4, dot3(pre_grad, pick, 1, 0), dot3(active, pick, 1, 0)
    )
    from_down = iota((2 * R, 256), 0) % 8 < 4
    for half in (1, 0):
        lanes = slice(256 * half, 256 * half + 256)
        g[half] = jnp.where(
            from_down,
            dot3(both, hid[:, lanes], 0, 0),
            dot3(both, cot_ref[:, lanes], 0, 0),
        ).reshape(NZ, NY, 8, 256)

    def send_half(z_first, half, ss, rs):
        out = []
        dst = zbuf if z_first else abuf
        for d in range(1, 8):
            if z_first:
                src = g.at[1, (z + d) % NZ, pl.ds(4 * half, 4)]
            else:
                src = g.at[0, pl.ds(4 * half, 4), (y + d) % NY]
            cp = rcopy(
                src, dst.at[d, pl.ds(4 * half, 4)], ss.at[d], rs.at[d],
                zdev(d) if z_first else ydev(d),
            )
            cp.start()
            out.append(cp)
        return out

    cb0 = send_half(True, 0, sc, rc)
    weighted = jnp.zeros(sq, f32)
    for p in range(4):
        xp, gp = x_ref[:, pairs[p]], ghs[:, pairs[p]]
        weighted = weighted + dmask[2 * p] * dot3(jnp.where(left, gp, 0.0), xp, 1, 1)
        weighted = weighted + dmask[2 * p + 1] * dot3(jnp.where(left, 0.0, gp), xp, 1, 1)
    cpart[...] = (dot3(weighted, b, 1, 0) + dot3(head_gh, state_in, 1, 0)).reshape(8, 16, 128)
    e5 = send_all(lambda d: cpart.at[(m + d) % NMOD], cbuf, t5, q5, mdev)
    arrive(e1)
    state, _ = row_prefix(True, y, gat2, gaux, pre, pdec)
    tot2[...] = state
    e3 = send_all(lambda d: tot2, zg2, t3, q3, zdev)
    cb1 = send_half(True, 1, sd, rd)
    ca0 = send_half(False, 0, sa, ra)
    zg2[0] = tot2[...]
    cacc[...] = add_up(cpart[m], e5, cbuf)
    e6 = send_all(lambda d: cacc, cag, t6, q6, mdev)
    out_ref[...] = hid[...] + dot3(active, up_ref[lang], 1, 0)
    b_part = dot3(weighted, c, 0, 0)
    arrive(e3)
    carry = row_carry(True, z, lambda i: zg2[i], lambda i: auxz[i][0:1])
    e4 = send_back(pre, carry, ret2, retin2, t4, q4)
    ca1 = send_half(False, 1, sb, rb)
    zbuf[0] = g[1, z]
    for t in range(NZ):
        abuf[0, t] = g[0, t, y]
    cag[0] = cacc[...]
    for p in range(4):
        gp = ghs[:, pairs[p]]
        ig_ref[:, pairs[p]] = (
            jnp.where(left, dot3(mix[2 * p], gp, 0, 0), dot3(mix[2 * p + 1], gp, 0, 0))
            + skip_ref[:, pairs[p]] * gp
        )
    arrive(e6)
    csum_ref[...] = in_order(cag, m)
    arrive(e4)
    adj = in_order(retin2, y)
    bpart[...] = (b_part + dot3(tailf[...] * x_ref[...], adj, 1, 0)).reshape(8, 16, 128)
    e7 = send_all(lambda d: bpart.at[(m + d) % NMOD], xbuf, t7, q7, mdev)
    ig_ref[...] = ig_ref[...] + tailf[...] * dot3(b, adj, 1, 1)
    xacc[...] = add_up(bpart[m], e7, xbuf)
    e8 = send_all(lambda d: xacc, xag, t8, q8, mdev)
    xag[0] = xacc[...]
    arrive(cb0 + cb1)
    by_lang(zbuf, auxz, zpart)
    ce = send_all(lambda d: zpart.at[(y + d) % NY], zybuf, se, re, ydev)
    arrive(ca0 + ca1)
    by_lang(abuf, gaux, apart)
    cf = send_all(lambda d: apart.at[(z + d) % NZ], azbuf, sf, rf, zdev)
    arrive(e8)
    bsum_ref[...] = in_order(xag, m)
    wg[:, :, 256:] = add_up(zpart[y], ce, zybuf)
    wg[:, :, :256] = add_up(apart[z], cf, azbuf)
    downg_ref[...] = wg[:, 0:4, :]
    upg_ref[...] = wg[:, 4:8, :]
    for cp in c1 + c2 + c3 + c4 + c5 + c6 + c7 + c8 + e1 + e3 + e4 + e5 + e6 + e7 + e8:
        cp.wait_send()
    for cp in ca0 + ca1 + cb0 + cb1 + ce + cf:
        cp.wait_send()


def vmem(*shape):
    return pltpu.VMEM(shape, f32)


def out_of(*shape):
    return jax.ShapeDtypeStruct(shape, f32)


def layer_call(*args):
    st, tile, wide = (8, P_SIZE, 128), (8, 8, 128), (128, 512)
    act, proj = (8, 16, R), (8, 16, 128)
    big, mid = (8, 8, 8, 256), (8, LANG, 8, 256)
    shapes = [
        st, tile, st, tile, st, tile, (P_SIZE + 8, 128), (8, P_SIZE + 8, 128), st, st,
        act, act, act[1:], act, act, act, act[1:], act,
        st, st, st[1:], st, st, st,
        (2,) + big, big, mid, mid, big, mid, mid, tile,
        proj, proj, proj[1:], proj, proj, proj, proj[1:], proj,
        (8, 128, 128), (8, 128, 128), wide, wide, wide, wide, (LANG, 8, 512),
    ]
    return pl.pallas_call(
        layer_kernel,
        name="layer",
        out_shape=(
            out_of(*wide), out_of(*wide), out_of(128, 128), out_of(128, 128),
            out_of(LANG, 4, 512), out_of(LANG, 4, 512),
        ),
        in_specs=[pl.BlockSpec(memory_space=pltpu.SMEM)] + [VM] * 8,
        out_specs=(VM,) * 6,
        scratch_shapes=[vmem(*s) for s in shapes] + [DMA((8,))] * 42,
        compiler_params=pltpu.CompilerParams(collective_id=1, has_side_effects=True),
    )(*args)


def shards(
    seq_input, log_decay, b_proj, c_proj, skip_gain, down_weight, up_weight, block_lang, cotangent
):
    skip = jnp.repeat(skip_gain, P_SIZE)[None, :]
    layer_out, input_grad, b_grad, c_grad, down_t, up_grad = layer_call(
        block_lang, seq_input, log_decay, b_proj, c_proj, skip, down_weight, up_weight, cotangent
    )
    return layer_out, input_grad, b_grad, c_grad, down_t.transpose(0, 2, 1), up_grad


def solution(mesh):
    return jax.shard_map(
        shards,
        mesh=mesh,
        in_specs=(
            P("ctx", "mod"),
            P("mod", "ctx"),
            P("ctx", None),
            P("ctx", None),
            P("mod"),
            P(None, "mod", None),
            P(None, None, "mod"),
            P("ctx"),
            P("ctx", "mod"),
        ),
        out_specs=(
            P("ctx", "mod"),
            P("ctx", "mod"),
            P("ctx", None),
            P("ctx", None),
            P(None, "mod", "ctx"),
            P(None, "ctx", "mod"),
        ),
        check_vma=False,
    )
```

```python
import jax
import jax.numpy as jnp
from jax import lax
from jax.experimental import pallas as pl
from jax.experimental.pallas import tpu as pltpu
from jax.sharding import PartitionSpec as P

P_SIZE = 64
R = 256
LANG = 2
NY = 8
NZ = 8
NMOD = 8
HALF = 32
f32 = jnp.float32
MESH = pl.DeviceIdType.MESH
VM = pl.BlockSpec(memory_space=pltpu.VMEM)
SM = pl.BlockSpec(memory_space=pltpu.SMEM)
DMA = pltpu.SemaphoreType.DMA


def rcopy(src, dst, ss, rs, dev):
    return pltpu.make_async_remote_copy(
        src_ref=src, dst_ref=dst, send_sem=ss, recv_sem=rs, device_id=dev, device_id_type=MESH
    )


def ctx_place():
    c = lax.axis_index("ctx")
    return c // NY, c % NY, lax.axis_index("mod")


def y_dev(z, y, d):
    return {"ctx": z * NY + (y + d) % NY}


def z_dev(z, y, d):
    return {"ctx": ((z + d) % NZ) * NY + y}


def m_dev(m, d):
    return {"mod": (m + d) % NMOD}


def greet(z, y, m):
    barrier = pltpu.get_barrier_semaphore()
    for d in range(1, 8):
        for dev in (y_dev(z, y, d), z_dev(z, y, d), m_dev(m, d)):
            pl.semaphore_signal(barrier, inc=1, device_id=dev, device_id_type=MESH)


def dot3(a, b, ca, cb):
    def split(v):
        top = v.astype(jnp.bfloat16)
        return top, (v - top.astype(f32)).astype(jnp.bfloat16)

    def one(p, q):
        return lax.dot_general(p, q, (((ca,), (cb,)), ((), ())), preferred_element_type=f32)

    (ah, al), (bh, bl) = split(a), split(b)
    return one(ah, bh) + (one(ah, bl) + one(al, bh))


def send_all(pick, dst, ss, rs, dev):
    out = []
    for d in range(1, 8):
        cp = rcopy(pick(d), dst.at[d], ss.at[d], rs.at[d], dev(d))
        cp.start()
        out.append(cp)
    return out


def arrive(copies):
    for cp in copies:
        cp.wait_recv()


def add_up(own, copies, buf):
    total = own
    for d in range(1, 8):
        copies[d - 1].wait_recv()
        total = total + buf[d]
    return total


def row_prefix(reverse, y, rows, gat, gaux, pre, pdec):
    state = jnp.zeros((HALF, 128), f32)
    dec = jnp.ones((1, 128), f32)
    for s in range(NY - 1, -1, -1) if reverse else range(NY):
        slot = (y - s + NY) % NY
        pre[s, rows] = state
        pdec[s] = jnp.broadcast_to(dec, (8, 128))
        dd = gaux[slot][0:1]
        state = dd * state + gat[slot, rows]
        dec = dd * dec
    return state, dec


def row_carry(reverse, z, rows, zg, auxz):
    carry = jnp.zeros((HALF, 128), f32)
    for s in range(NZ - 1, -1, -1) if reverse else range(NZ):
        slot = (z - s + NZ) % NZ
        nxt = auxz[slot][0:1] * carry + zg[slot, rows]
        use = (z < s) if reverse else (z > s)
        carry = jnp.where(use, nxt, carry)
    return carry


def by_lang(buf, aux, out):
    def body(t, _):
        a, b = jnp.zeros((8, 256), f32), jnp.zeros((8, 256), f32)
        for d in range(8):
            v = buf[d, t]
            first = jnp.broadcast_to(aux[d][1:2, 0:1], (8, 256)) < 0.5
            a = a + jnp.where(first, v, 0.0)
            b = b + jnp.where(first, 0.0, v)
        out[t, 0] = a
        out[t, 1] = b
        return 0

    lax.fori_loop(0, 8, body, 0)


def layer_kernel(
    lang_ref, x_ref, ld_ref, b_ref, c_ref, skip_ref, down_ref, up_ref, cot_ref,
    out_ref, ig_ref, bsum_ref, csum_ref, downg_ref, upg_ref,
    st, aux, gat, gaux, pre, pdec, tot, tile, zg, ret, retin,
    back, bbuf, bacc, bag, part, rbuf, racc, rag,
    st2, gat2, tot2, zg2, ret2, retin2,
    g, abuf, apart, azbuf, zbuf, zpart, zybuf, auxz,
    cpart, cbuf, cacc, cag, bpart, xbuf, xacc, xag,
    mix, dmask, hid, headf, tailf, ghs, wg,
    s1, r1, s3, r3, s4, r4, t1, q1, t3, q3, t4, q4,
    s2, r2, s9, r9, s5, r5, s6, r6, s7, r7, s8, r8, t5, q5, t6, q6, t7, q7, t8, q8,
    sa, ra, sb, rb, sc, rc, sd, rd, se, re, sf, rf,
):
    z, y, m = ctx_place()
    greet(z, y, m)
    ydev = lambda d: y_dev(z, y, d)
    zdev = lambda d: z_dev(z, y, d)
    mdev = lambda d: m_dev(m, d)
    lang = lang_ref[0]
    iota = lambda shape, dim: lax.broadcasted_iota(jnp.int32, shape, dim)
    sq = (128, 128)
    lower = iota(sq, 0) >= iota(sq, 1)
    left = iota(sq, 1) < P_SIZE
    halves = [pl.ds(HALF * k, HALF) for k in range(2)]

    def send_rows(pick, dst, ss, rs, dev, k):
        out = []
        for d in range(1, 8):
            cp = rcopy(pick(d, halves[k]), dst.at[d, halves[k]], ss.at[k, d], rs.at[k, d], dev(d))
            cp.start()
            out.append(cp)
        return out

    pairs = [slice(128 * p, 128 * p + 128) for p in range(4)]

    def spread(v, p):
        return jnp.where(
            left,
            jnp.broadcast_to(v[:, 2 * p : 2 * p + 1], sq),
            jnp.broadcast_to(v[:, 2 * p + 1 : 2 * p + 2], sq),
        )

    ones = lower.astype(f32)
    ld = ld_ref[...]
    full = lax.Precision.HIGHEST
    cum_row = lax.dot_general(
        ld, ones, (((1,), (1,)), ((), ())), precision=full, preferred_element_type=f32
    )
    cum_col = lax.dot_general(
        ones, ld, (((1,), (1,)), ((), ())), precision=full, preferred_element_type=f32
    )
    tail_c = jnp.exp(cum_col[127:128, :] - cum_col)
    head_c = jnp.exp(cum_col)
    for p in range(4):
        tailf[:, pairs[p]] = spread(tail_c, p)
        headf[:, pairs[p]] = spread(head_c, p)
    b, c = b_ref[...], c_ref[...]
    st[...] = dot3(tailf[...] * x_ref[...], b, 0, 0).reshape(8, P_SIZE, 128)
    total = jnp.exp(cum_row[:, 127:128])
    lang_tile = jnp.full((8, 128), lang.astype(f32), f32)
    top_row = iota((8, 128), 0) == 0
    for h in range(8):
        aux[h] = jnp.where(top_row, jnp.broadcast_to(total[h : h + 1, :], (8, 128)), lang_tile)
    pl.semaphore_wait(pltpu.get_barrier_semaphore(), 21)

    c2 = send_all(lambda d: aux.at[(y + d) % NY], gaux, s2, r2, ydev)
    c1 = [
        send_rows(lambda d, r: st.at[(y + d) % NY, r], gat, s1, r1, ydev, k) for k in range(2)
    ]
    gat[0] = st[y]
    gaux[0] = aux[y]
    back[...] = dot3(cot_ref[...], up_ref[lang], 1, 1).reshape(NMOD, 16, R)
    c5 = send_all(lambda d: back.at[(m + d) % NMOD], bbuf, s5, r5, mdev)
    scores = dot3(c, b, 1, 1)
    for p in range(4):
        xp = x_ref[:, pairs[p]]
        got = []
        for h in (2 * p, 2 * p + 1):
            gap = jnp.broadcast_to(cum_col[:, h : h + 1], sq) - jnp.broadcast_to(
                cum_row[h : h + 1, :], sq
            )
            dm = jnp.where(lower, jnp.exp(jnp.where(lower, gap, 0.0)), 0.0)
            dmask[h] = dm
            mix[h] = dm * scores
            got.append(dot3(mix[h], xp, 1, 0))
        hid[:, pairs[p]] = jnp.where(left, got[0], got[1]) + jnp.where(left, skip_ref[2 * p], skip_ref[2 * p + 1]) * xp
    arrive(c2)
    c3, c4, c9 = [], [], []
    for k in range(2):
        arrive(c1[k])
        state, dec = row_prefix(False, y, halves[k], gat, gaux, pre, pdec)
        if k == 0:
            tile[...] = jnp.where(top_row, jnp.broadcast_to(dec, (8, 128)), lang_tile)
            c9 = send_all(lambda d: tile, auxz, s9, r9, zdev)
        tot[halves[k]] = state
        c3.append(send_rows(lambda d, r: tot.at[r], zg, s3, r3, zdev, k))
    bacc[...] = add_up(back[m], c5, bbuf)
    c6 = send_all(lambda d: bacc, bag, s6, r6, mdev)
    zg[0] = tot[...]
    bag[0] = bacc[...]
    auxz[0] = tile[...]
    arrive(c9)

    def send_back(k, carry, ret, retin, ss, rs):
        r = halves[k]
        out = []
        for d in range(1, NY):
            s = (y + d) % NY
            ret[d, r] = pre[s, r] + pdec[s][0:1] * carry
            cp = rcopy(ret.at[d, r], retin.at[d, r], ss.at[k, d], rs.at[k, d], ydev(d))
            cp.start()
            out.append(cp)
        retin[0, r] = pre[y, r] + pdec[y][0:1] * carry
        return out

    def in_order(buf, place):
        return jnp.concatenate([buf[(place - h + 8) % 8] for h in range(8)], axis=0)

    for k in range(2):
        arrive(c3[k])
        carry = row_carry(False, z, halves[k], zg, auxz)
        c4 += send_back(k, carry, ret, retin, s4, r4)
    arrive(c6)
    back_act = in_order(bag, m)
    arrive(c4)
    state_in = in_order(retin, y)
    hid[...] = hid[...] + headf[...] * dot3(c, state_in, 1, 1)
    part[...] = dot3(hid[...], down_ref[lang], 1, 0).reshape(NMOD, 16, R)
    c7 = send_all(lambda d: part.at[(m + d) % NMOD], rbuf, s7, r7, mdev)
    racc[...] = add_up(part[m], c7, rbuf)
    c8 = send_all(lambda d: racc, rag, s8, r8, mdev)
    rag[0] = racc[...]
    arrive(c8)
    pre_act = in_order(rag, m)
    gate = jax.nn.sigmoid(pre_act)
    active = pre_act * gate
    pre_grad = back_act * (gate * (1.0 + pre_act * (1.0 - gate)))

    gh = cot_ref[...] + dot3(pre_grad, down_ref[lang], 1, 1)
    ghs[...] = gh
    head_gh = headf[...] * gh
    st2[...] = dot3(head_gh, c, 0, 0).reshape(8, P_SIZE, 128)
    e1 = [
        send_rows(lambda d, r: st2.at[(y + d) % NY, r], gat2, t1, q1, ydev, k) for k in range(2)
    ]
    gat2[0] = st2[y]

    col = iota((R, 2 * R), 1)
    pick = (iota((R, 2 * R), 0) == 4 * (col // 8) + col % 4).astype(f32)
    both = jnp.where(
        iota((128, 2 * R), 1) % 8 < 4, dot3(pre_grad, pick, 1, 0), dot3(active, pick, 1, 0)
    )
    from_down = iota((2 * R, 256), 0) % 8 < 4
    for half in (1, 0):
        lanes = slice(256 * half, 256 * half + 256)
        g[half] = jnp.where(
            from_down,
            dot3(both, hid[:, lanes], 0, 0),
            dot3(both, cot_ref[:, lanes], 0, 0),
        ).reshape(NZ, NY, 8, 256)

    def send_half(z_first, half, ss, rs):
        out = []
        dst = zbuf if z_first else abuf
        for d in range(1, 8):
            if z_first:
                src = g.at[1, (z + d) % NZ, pl.ds(4 * half, 4)]
            else:
                src = g.at[0, pl.ds(4 * half, 4), (y + d) % NY]
            cp = rcopy(
                src, dst.at[d, pl.ds(4 * half, 4)], ss.at[d], rs.at[d],
                zdev(d) if z_first else ydev(d),
            )
            cp.start()
            out.append(cp)
        return out

    cb0 = send_half(True, 0, sc, rc)
    weighted = jnp.zeros(sq, f32)
    for p in range(4):
        xp, gp = x_ref[:, pairs[p]], ghs[:, pairs[p]]
        weighted = weighted + dmask[2 * p] * dot3(jnp.where(left, gp, 0.0), xp, 1, 1)
        weighted = weighted + dmask[2 * p + 1] * dot3(jnp.where(left, 0.0, gp), xp, 1, 1)
    cpart[...] = (dot3(weighted, b, 1, 0) + dot3(head_gh, state_in, 1, 0)).reshape(8, 16, 128)
    e5 = send_all(lambda d: cpart.at[(m + d) % NMOD], cbuf, t5, q5, mdev)
    e3, e4 = [], []
    for k in range(2):
        arrive(e1[k])
        tot2[halves[k]], _ = row_prefix(True, y, halves[k], gat2, gaux, pre, pdec)
        e3.append(send_rows(lambda d, r: tot2.at[r], zg2, t3, q3, zdev, k))
    cb1 = send_half(True, 1, sd, rd)
    ca0 = send_half(False, 0, sa, ra)
    zg2[0] = tot2[...]
    cacc[...] = add_up(cpart[m], e5, cbuf)
    e6 = send_all(lambda d: cacc, cag, t6, q6, mdev)
    out_ref[...] = hid[...] + dot3(active, up_ref[lang], 1, 0)
    b_part = dot3(weighted, c, 0, 0)
    for k in range(2):
        arrive(e3[k])
        carry = row_carry(True, z, halves[k], zg2, auxz)
        e4 += send_back(k, carry, ret2, retin2, t4, q4)
    ca1 = send_half(False, 1, sb, rb)
    zbuf[0] = g[1, z]
    for t in range(NZ):
        abuf[0, t] = g[0, t, y]
    cag[0] = cacc[...]
    for p in range(4):
        gp = ghs[:, pairs[p]]
        ig_ref[:, pairs[p]] = (
            jnp.where(left, dot3(mix[2 * p], gp, 0, 0), dot3(mix[2 * p + 1], gp, 0, 0))
            + jnp.where(left, skip_ref[2 * p], skip_ref[2 * p + 1]) * gp
        )
    arrive(e6)
    csum_ref[...] = in_order(cag, m)
    arrive(e4)
    adj = in_order(retin2, y)
    bpart[...] = (b_part + dot3(tailf[...] * x_ref[...], adj, 1, 0)).reshape(8, 16, 128)
    e7 = send_all(lambda d: bpart.at[(m + d) % NMOD], xbuf, t7, q7, mdev)
    ig_ref[...] = ig_ref[...] + tailf[...] * dot3(b, adj, 1, 1)
    xacc[...] = add_up(bpart[m], e7, xbuf)
    e8 = send_all(lambda d: xacc, xag, t8, q8, mdev)
    xag[0] = xacc[...]
    arrive(cb0 + cb1)
    by_lang(zbuf, auxz, zpart)
    ce = send_all(lambda d: zpart.at[(y + d) % NY], zybuf, se, re, ydev)
    arrive(ca0 + ca1)
    by_lang(abuf, gaux, apart)
    cf = send_all(lambda d: apart.at[(z + d) % NZ], azbuf, sf, rf, zdev)
    arrive(e8)
    bsum_ref[...] = in_order(xag, m)
    wg[:, :, 256:] = add_up(zpart[y], ce, zybuf)
    wg[:, :, :256] = add_up(apart[z], cf, azbuf)
    downg_ref[...] = wg[:, 0:4, :]
    upg_ref[...] = wg[:, 4:8, :]
    for cp in c1[0] + c1[1] + c2 + c3[0] + c3[1] + c4 + c5 + c6 + c7 + c8 + c9:
        cp.wait_send()
    for cp in e1[0] + e1[1] + e3[0] + e3[1] + e4 + e5 + e6 + e7 + e8:
        cp.wait_send()
    for cp in ca0 + ca1 + cb0 + cb1 + ce + cf:
        cp.wait_send()


def vmem(*shape):
    return pltpu.VMEM(shape, f32)


def out_of(*shape):
    return jax.ShapeDtypeStruct(shape, f32)


def layer_call(*args):
    st, tile, wide = (8, P_SIZE, 128), (8, 8, 128), (128, 512)
    act, proj = (8, 16, R), (8, 16, 128)
    big, mid = (8, 8, 8, 256), (8, LANG, 8, 256)
    shapes = [
        st, tile, st, tile, st, tile, st[1:], tile[1:], st, st, st,
        act, act, act[1:], act, act, act, act[1:], act,
        st, st, st[1:], st, st, st,
        (2,) + big, big, mid, mid, big, mid, mid, tile,
        proj, proj, proj[1:], proj, proj, proj, proj[1:], proj,
        (8, 128, 128), (8, 128, 128), wide, wide, wide, wide, (LANG, 8, 512),
    ]
    return pl.pallas_call(
        layer_kernel,
        name="layer",
        out_shape=(
            out_of(*wide), out_of(*wide), out_of(128, 128), out_of(128, 128),
            out_of(LANG, 4, 512), out_of(LANG, 4, 512),
        ),
        in_specs=[SM] + [VM] * 4 + [SM] + [VM] * 3,
        out_specs=(VM,) * 6,
        scratch_shapes=[vmem(*s) for s in shapes] + [DMA((2, 8))] * 12 + [DMA((8,))] * 32,
        compiler_params=pltpu.CompilerParams(collective_id=1, has_side_effects=True),
    )(*args)


def shards(
    seq_input, log_decay, b_proj, c_proj, skip_gain, down_weight, up_weight, block_lang, cotangent
):
    layer_out, input_grad, b_grad, c_grad, down_t, up_grad = layer_call(
        block_lang, seq_input, log_decay, b_proj, c_proj, skip_gain, down_weight, up_weight, cotangent
    )
    return layer_out, input_grad, b_grad, c_grad, down_t.transpose(0, 2, 1), up_grad


def solution(mesh):
    return jax.shard_map(
        shards,
        mesh=mesh,
        in_specs=(
            P("ctx", "mod"),
            P("mod", "ctx"),
            P("ctx", None),
            P("ctx", None),
            P("mod"),
            P(None, "mod", None),
            P(None, None, "mod"),
            P("ctx"),
            P("ctx", "mod"),
        ),
        out_specs=(
            P("ctx", "mod"),
            P("ctx", "mod"),
            P("ctx", None),
            P("ctx", None),
            P(None, "mod", "ctx"),
            P(None, "ctx", "mod"),
        ),
        check_vma=False,
    )
```
